32 devices in a mesh: ax: 4 (over x, core), rad: 8 (over z, y).
Axes of the slice: x: 2, y: 2, z: 4, core: 2. Of those that a mesh axis runs over, the one named last changes fastest.
Arguments:
- sources: float32 [8, 16, 200, 128], P('ax', 'rad'), may hold values from -0.6 to 0.6
- block_inverse: float32 [8, 16, 200, 200], P('ax', 'rad'), may hold values from -2 to 2, as said below
- radial_coupling: float32 [8, 16, 2, 200], P('ax', 'rad'), may hold values from 0.2 to 1.2
- axial_coupling: float32 [8, 16, 4, 200], P('ax', 'rad'), may hold values from 0.01 to 0.05
Outputs:
- correction: float32 [8, 16, 200, 128], P('ax', 'rad')
The draws below stay inside these ranges and needn't reach their ends.
Inputs may be any that keep to these rules, and one draw needn't show every extreme that they name: `block_inverse`: the given inverse of each cell's diagonal block.
All inputs are finite; a program needn't handle non-finite values.
Results may differ from the reference program's by a relative error of at most 0.00014.
Values sent between devices are 32-bit elements; how exact they have to be, the bound alone decides.
A program may use at most 64 MiB of HBM per device.

```python
import math
import jax
import jax.numpy as jnp
from jax import lax

S = 200
K = 128
SWEEPS = 2
NA = 8
NR = 16


def draw_block_inverse(key, part):
    key_diag, key_off = jax.random.split(jax.random.fold_in(key, 11), 2)
    diagonal = jax.random.uniform(key_diag, (NA, NR, S), jnp.float32, 0.8, 1.2)
    spread = jax.random.normal(key_off, (NA, NR, S, S), jnp.float32) * (0.25 / math.sqrt(S))
    spread = jnp.clip(spread, -0.5, 0.5)
    return spread + diagonal[..., None] * jnp.eye(S, dtype=jnp.float32)


def draw_radial_coupling(key, part):
    key_rate, key_rough = jax.random.split(jax.random.fold_in(key, 23), 2)
    species_rate = jax.random.uniform(key_rate, (2, S), jnp.float32, 0.35, 0.9)
    roughness = jax.random.uniform(key_rough, (NA, NR, 2, S), jnp.float32, 0.65, 1.3)
    return species_rate * roughness


def block_levels(stream_key, extent, cuts, least, high):
    loudness = 1.0
    for dim, parts in cuts:
        heights = jax.random.uniform(jax.random.fold_in(jax.random.fold_in(stream_key, 6), dim), (parts,), jnp.float32, least / len(cuts), high / len(cuts))
        loudness = loudness * jnp.repeat(jnp.exp(heights), extent[dim] // parts).reshape((-1,) + (1,) * (len(extent) - 1 - dim))
    return loudness


def normal_values(own_key, dims, width, bound, shards=(), kind=jnp.bfloat16):
    values = jax.random.normal(own_key, dims, jnp.float32) * width
    if len(shards) > 0:
        values = block_levels(own_key, dims, shards, -0.22, 0.18) * values
    return jnp.clip(values, min=-bound, max=bound).astype(kind)


def setup_inputs(seed: int = 0) -> dict:
    streams_of = jax.random.split(jax.random.key(seed), 5)
    sources = normal_values(streams_of[0], (NA, NR, S, K), 0.1, 0.6, ((0, 4), (1, 8)), jnp.float32)
    block_inverse = draw_block_inverse(jax.random.fold_in(streams_of[4], 71), 0)
    radial_coupling = draw_radial_coupling(jax.random.fold_in(streams_of[4], 71), 0)
    axial_coupling = jnp.clip(0.01 + 0.04 * jax.random.uniform(streams_of[3], (NA, NR, 4, S), jnp.float32) ** block_levels(streams_of[3], (NA, NR, 4, S), ((0, 4), (1, 8)), -0.2, 0.2), 0.01, 0.05)
    return {"sources": sources, "block_inverse": block_inverse, "radial_coupling": radial_coupling, "axial_coupling": axial_coupling}


def forward_line(line_source, block_inverse, inward_coupling):
    def advance(previous, entries):
        source_row, inverse_row, coupling_row = entries
        shifted = source_row - coupling_row[..., None] * previous
        current = jnp.einsum('aij,ajk->aik', inverse_row, shifted, precision=lax.Precision.HIGHEST)
        return current, current
    initial = jnp.zeros((NA, S, K), jnp.float32)
    _, values = lax.scan(advance, initial, (jnp.moveaxis(line_source, 1, 0), jnp.moveaxis(block_inverse, 1, 0), jnp.moveaxis(inward_coupling, 1, 0)))
    return jnp.moveaxis(values, 0, 1)


def backward_line(inner_value, block_inverse, outward_coupling):
    def retreat(following, entries):
        inner_row, inverse_row, coupling_row = entries
        shifted = coupling_row[..., None] * following
        current = inner_row - jnp.einsum('aij,ajk->aik', inverse_row, shifted, precision=lax.Precision.HIGHEST)
        return current, current
    initial = jnp.zeros((NA, S, K), jnp.float32)
    _, values = lax.scan(retreat, initial, (jnp.moveaxis(inner_value, 1, 0), jnp.moveaxis(block_inverse, 1, 0), jnp.moveaxis(outward_coupling, 1, 0)), reverse=True)
    return jnp.moveaxis(values, 0, 1)


def reference(sources, block_inverse, radial_coupling, axial_coupling):
    correction = jnp.zeros((NA, NR, S, K), jnp.float32)
    for sweep_index in range(SWEEPS):
        if sweep_index == 0:
            line_source = sources
        else:
            padded = jnp.pad(correction, ((2, 2), (0, 0), (0, 0), (0, 0)))
            line_source = sources
            line_source = line_source - axial_coupling[:, :, 0, :, None] * padded[0:NA]
            line_source = line_source - axial_coupling[:, :, 1, :, None] * padded[1:NA + 1]
            line_source = line_source - axial_coupling[:, :, 2, :, None] * padded[3:NA + 3]
            line_source = line_source - axial_coupling[:, :, 3, :, None] * padded[4:NA + 4]
        inner_value = forward_line(line_source, block_inverse, radial_coupling[:, :, 0])
        correction = backward_line(inner_value, block_inverse, radial_coupling[:, :, 1])
    return correction
```

```python
import functools
import jax
import jax.numpy as jnp
from jax import lax
from jax.experimental import pallas as pl
from jax.experimental.pallas import tpu as pltpu
from jax.sharding import PartitionSpec as P

SWEEPS = 2
WIDTH = 2
MESH = pl.DeviceIdType.MESH


def split(value):
    high = value.astype(jnp.bfloat16)
    low = (value - high.astype(jnp.float32)).astype(jnp.bfloat16)
    return high, low


def keep(ref, index, value):
    high, low = split(value)
    ref[index + (0,)] = high
    ref[index + (1,)] = low


def apply(ref, index, operand):
    high, low = split(operand)
    left_high = ref[index + (0,)]
    left_low = ref[index + (1,)]
    dot = functools.partial(jnp.dot, preferred_element_type=jnp.float32)
    return dot(left_high, high) + (dot(left_high, low) + dot(left_low, high))


def kernel(
    segments,
    blocks,
    sources,
    inverse,
    radial,
    axial,
    out,
    plain,
    inner,
    outer,
    chain,
    line,
    value,
    field,
    low,
    high,
    arriving,
    leaving,
    send_sem,
    recv_sem,
    side_send,
    side_recv,
):
    stations, cells = sources.shape[:2]
    rad = lax.axis_index("rad")
    ax = lax.axis_index("ax")
    rad_up, rad_down = rad < segments - 1, rad > 0
    ax_up, ax_down = ax < blocks - 1, ax > 0

    barrier = pltpu.get_barrier_semaphore()
    neighbours = (
        (rad_up, {"rad": rad + 1}),
        (rad_down, {"rad": rad - 1}),
        (ax_up, {"ax": ax + 1}),
        (ax_down, {"ax": ax - 1}),
    )
    for exists, device in neighbours:

        @pl.when(exists)
        def _():
            pl.semaphore_signal(barrier, inc=1, device_id=device, device_id_type=MESH)

    peers = sum(jnp.where(exists, 1, 0) for exists, device in neighbours)
    pl.semaphore_wait(barrier, peers)

    def hop(number, station, step):
        return pltpu.make_async_remote_copy(
            src_ref=leaving.at[number, station],
            dst_ref=arriving.at[number, station],
            send_sem=send_sem.at[number, station],
            recv_sem=recv_sem.at[number, station],
            device_id={"rad": rad + step},
            device_id_type=MESH,
        )

    def side(direction):
        block = field.at[pl.ds(stations - WIDTH, WIDTH)] if direction == 0 else field.at[pl.ds(0, WIDTH)]
        return pltpu.make_async_remote_copy(
            src_ref=block,
            dst_ref=low if direction == 0 else high,
            send_sem=side_send.at[direction],
            recv_sem=side_recv.at[direction],
            device_id={"ax": ax + 1 if direction == 0 else ax - 1},
            device_id_type=MESH,
        )

    @pl.when(jnp.logical_not(rad_down))
    def _():
        for number in range(0, 2 * SWEEPS, 2):
            arriving[number] = jnp.zeros(arriving.shape[1:], jnp.float32)

    @pl.when(jnp.logical_not(rad_up))
    def _():
        for number in range(1, 2 * SWEEPS, 2):
            arriving[number] = jnp.zeros(arriving.shape[1:], jnp.float32)

    @pl.when(jnp.logical_not(ax_down))
    def _():
        low[...] = jnp.zeros(low.shape, jnp.float32)

    @pl.when(jnp.logical_not(ax_up))
    def _():
        high[...] = jnp.zeros(high.shape, jnp.float32)

    for a in range(stations):
        for c in range(cells):
            block = inverse[a, c]
            keep(plain, (a, c), block)
            keep(inner, (a, c), block * radial[a, c, 0:1, :])
            keep(outer, (a, c), block * radial[a, c, 1:2, :])
        product = -(inverse[a, 0] * radial[a, 0, 0:1, :])
        for c in range(1, cells):
            product = -apply(inner, (a, c), product)
        keep(chain, (0, a), product)
        product = -(inverse[a, cells - 1] * radial[a, cells - 1, 1:2, :])
        for c in reversed(range(cells - 1)):
            product = -apply(outer, (a, c), product)
        keep(chain, (1, a), product)

    for sweep in range(SWEEPS):
        if sweep == 0:
            source = sources
        else:

            @pl.when(ax_down)
            def _():
                side(0).wait_recv()

            @pl.when(ax_up)
            def _():
                side(1).wait_recv()

            for a in range(stations):
                for c in range(cells):
                    total = sources[a, c]
                    for j, place in enumerate((0, 1, 3, 4)):
                        at = a + place
                        if at < WIDTH:
                            other = low[at, c]
                        elif at < WIDTH + stations:
                            other = field[at - WIDTH, c]
                        else:
                            other = high[at - WIDTH - stations, c]
                        k = (a * cells + c) * 4 + j
                        total = total - axial[:, k : k + 1] * other
                    line[a, c] = total
            source = line
        number = 2 * sweep
        for a in range(stations):
            previous = apply(plain, (a, 0), source[a, 0])
            value[a, 0] = previous
            for c in range(1, cells):
                previous = apply(plain, (a, c), source[a, c]) - apply(inner, (a, c), previous)
                value[a, c] = previous
        for a in range(stations):

            @pl.when(rad_down)
            def _():
                hop(number, a, 1).wait_recv()

            @pl.when(rad_up)
            def _():
                leaving[number, a] = value[a, cells - 1] + apply(chain, (0, a), arriving[number, a])
                hop(number, a, 1).start()

        for a in range(stations):
            change = -apply(inner, (a, 0), arriving[number, a])
            value[a, 0] += change
            for c in range(1, cells):
                change = -apply(inner, (a, c), change)
                value[a, c] += change
        number = 2 * sweep + 1
        firsts = []
        for a in range(stations):
            following = value[a, cells - 1]
            for c in reversed(range(cells - 1)):
                following = value[a, c] - apply(outer, (a, c), following)
            firsts.append(following)
        for a in range(stations):

            @pl.when(rad_up)
            def _():
                hop(number, a, -1).wait_recv()

            @pl.when(rad_down)
            def _():
                leaving[number, a] = firsts[a] + apply(chain, (1, a), arriving[number, a])
                hop(number, a, -1).start()

        target = field if sweep < SWEEPS - 1 else out
        for a in range(stations):
            following = arriving[number, a]
            for c in reversed(range(cells)):
                following = value[a, c] - apply(outer, (a, c), following)
                target[a, c] = following
        if sweep < SWEEPS - 1:

            @pl.when(ax_up)
            def _():
                side(0).start()

            @pl.when(ax_down)
            def _():
                side(1).start()

    for number in range(2 * SWEEPS):
        for a in range(stations):

            @pl.when(rad_up if number % 2 == 0 else rad_down)
            def _():
                hop(number, a, 1 if number % 2 == 0 else -1).wait_send()

    @pl.when(ax_up)
    def _():
        side(0).wait_send()

    @pl.when(ax_down)
    def _():
        side(1).wait_send()


def on_device(segments, blocks, sources, block_inverse, radial_coupling, axial_coupling):
    stations, cells, species, columns = sources.shape
    axial = axial_coupling.reshape(-1, species).T
    matrix = pltpu.VMEM((stations, cells, 2, species, species), jnp.bfloat16)
    grid = pltpu.VMEM((stations, cells, species, columns), jnp.float32)
    edge = pltpu.VMEM((WIDTH, cells, species, columns), jnp.float32)
    slots = pltpu.VMEM((2 * SWEEPS, stations, species, columns), jnp.float32)
    spec = pl.BlockSpec(memory_space=pltpu.VMEM)
    return pl.pallas_call(
        functools.partial(kernel, segments, blocks),
        out_shape=jax.ShapeDtypeStruct(sources.shape, jnp.float32),
        in_specs=[spec] * 4,
        out_specs=spec,
        scratch_shapes=[
            matrix,
            matrix,
            matrix,
            pltpu.VMEM((2, stations, 2, species, species), jnp.bfloat16),
            grid,
            grid,
            grid,
            edge,
            edge,
            slots,
            slots,
            pltpu.SemaphoreType.DMA((2 * SWEEPS, stations)),
            pltpu.SemaphoreType.DMA((2 * SWEEPS, stations)),
            pltpu.SemaphoreType.DMA((2,)),
            pltpu.SemaphoreType.DMA((2,)),
        ],
        compiler_params=pltpu.CompilerParams(
            collective_id=0, has_side_effects=True, vmem_limit_bytes=40 << 20
        ),
    )(sources, block_inverse, radial_coupling, axial)


def solution(mesh):
    placed = P("ax", "rad", None, None)
    return jax.shard_map(
        functools.partial(on_device, mesh.shape["rad"], mesh.shape["ax"]),
        mesh=mesh,
        in_specs=(placed,) * 4,
        out_specs=placed,
        check_vma=False,
    )
```

```python
import functools
import jax
import jax.numpy as jnp
from jax import lax
from jax.experimental import pallas as pl
from jax.experimental.pallas import tpu as pltpu
from jax.sharding import PartitionSpec as P

SWEEPS = 2
WIDTH = 2
MESH = pl.DeviceIdType.MESH


def split(value):
    high = value.astype(jnp.bfloat16)
    low = (value - high.astype(jnp.float32)).astype(jnp.bfloat16)
    return high, low


def keep(ref, index, value):
    high, low = split(value)
    ref[index + (0,)] = high
    ref[index + (1,)] = low


def apply(ref, index, operand):
    high, low = split(operand)
    left_high = ref[index + (0,)]
    left_low = ref[index + (1,)]
    dot = functools.partial(jnp.dot, preferred_element_type=jnp.float32)
    return dot(left_high, high) + (dot(left_high, low) + dot(left_low, high))


def kernel(
    segments,
    blocks,
    sources,
    inverse,
    radial,
    axial,
    out,
    plain,
    inner,
    outer,
    pair,
    sent_matrix,
    got_matrix,
    own_matrix,
    line,
    value,
    field,
    low,
    high,
    sent,
    got,
    local,
    arriving,
    leaving,
    matrix_send,
    matrix_recv,
    pair_send,
    pair_recv,
    hop_send,
    hop_recv,
    side_send,
    side_recv,
):
    stations, cells = sources.shape[:2]
    half = stations // 2
    rad = lax.axis_index("rad")
    ax = lax.axis_index("ax")
    parity = lax.rem(rad, 2)
    is_first = parity == 0
    top, bottom = rad >= segments - 2, rad < 2
    has_up, has_down = jnp.logical_not(top), jnp.logical_not(bottom)
    ax_up, ax_down = ax < blocks - 1, ax > 0
    partner = {"rad": rad + 1 - 2 * parity}
    mine = [parity * half + i for i in range(half)]
    other = [(1 - parity) * half + i for i in range(half)]

    barrier = pltpu.get_barrier_semaphore()
    neighbours = (
        (has_up, {"rad": rad + 2}),
        (has_down, {"rad": rad - 2}),
        (ax_up, {"ax": ax + 1}),
        (ax_down, {"ax": ax - 1}),
    )
    pl.semaphore_signal(barrier, inc=1, device_id=partner, device_id_type=MESH)
    for exists, device in neighbours:

        @pl.when(exists)
        def _():
            pl.semaphore_signal(barrier, inc=1, device_id=device, device_id_type=MESH)

    def remote(source, target, send_sem, recv_sem, device):
        return pltpu.make_async_remote_copy(
            src_ref=source,
            dst_ref=target,
            send_sem=send_sem,
            recv_sem=recv_sem,
            device_id=device,
            device_id_type=MESH,
        )

    def swap_matrix(kind, i):
        at = (kind, i)
        return remote(
            sent_matrix.at[at], got_matrix.at[at], matrix_send.at[at], matrix_recv.at[at], partner
        )

    def swap(sweep, kind, i):
        at = (sweep, kind, i)
        return remote(sent.at[at], got.at[at], pair_send.at[at], pair_recv.at[at], partner)

    def hop(number, i):
        at = (number, i)
        device = {"rad": rad + 2 if number % 2 == 0 else rad - 2}
        return remote(leaving.at[at], arriving.at[at], hop_send.at[at], hop_recv.at[at], device)

    def side(direction, station):
        at = (direction, station)
        device = {"ax": ax + 1 if direction == 0 else ax - 1}
        target = low if direction == 0 else high
        return remote(
            field.at[station], target.at[station], side_send.at[at], side_recv.at[at], device
        )

    @pl.when(bottom)
    def _():
        for number in range(0, 2 * SWEEPS, 2):
            arriving[number] = jnp.zeros(arriving.shape[1:], jnp.float32)

    @pl.when(top)
    def _():
        for number in range(1, 2 * SWEEPS, 2):
            arriving[number] = jnp.zeros(arriving.shape[1:], jnp.float32)

    @pl.when(jnp.logical_not(ax_down))
    def _():
        low[...] = jnp.zeros(low.shape, jnp.float32)

    @pl.when(jnp.logical_not(ax_up))
    def _():
        high[...] = jnp.zeros(high.shape, jnp.float32)

    def forms(a):
        for c in range(cells):
            block = inverse[a, c]
            keep(plain, (a, c), block)
            keep(inner, (a, c), block * radial[a, c, 0:1, :])
            keep(outer, (a, c), block * radial[a, c, 1:2, :])

    def inner_responses(a):
        answers = [-(inverse[a, 0] * radial[a, 0, 0:1, :])]
        for c in range(1, cells):
            answers.append(-apply(inner, (a, c), answers[-1]))
        return answers

    def other_responses(a, answers):
        turned = answers[-1]
        product = -(inverse[a, cells - 1] * radial[a, cells - 1, 1:2, :])
        for c in reversed(range(cells - 1)):
            turned = answers[c] - apply(outer, (a, c), turned)
            product = -apply(outer, (a, c), product)
        return turned, product

    def first_guess(source, a):
        previous = apply(plain, (a, 0), source[a, 0])
        value[a, 0] = previous
        for c in range(1, cells):
            previous = apply(plain, (a, c), source[a, c]) - apply(inner, (a, c), previous)
            value[a, c] = previous
        return previous

    def first_turn(a):
        following = value[a, cells - 1]
        for c in reversed(range(cells - 1)):
            following = value[a, c] - apply(outer, (a, c), following)
        return following

    def inner_update(a, incoming):
        change = -apply(inner, (a, 0), incoming)
        value[a, 0] += change
        for c in range(1, cells):
            change = -apply(inner, (a, c), change)
            value[a, c] += change

    def outer_finish(target, a, incoming):
        following = incoming
        for c in reversed(range(cells)):
            following = value[a, c] - apply(outer, (a, c), following)
            target[a, c] = following

    def ordered(own, foreign):
        return jnp.where(is_first, own, foreign), jnp.where(is_first, foreign, own)

    for i in range(half):
        forms(other[i])
    kept = [inner_responses(other[i]) for i in range(half)]
    for i in range(half):
        sent_matrix[0, i] = kept[i][-1]
    peers = 1 + sum(jnp.where(exists, 1, 0) for exists, device in neighbours)
    pl.semaphore_wait(barrier, peers)
    for i in range(half):
        swap_matrix(0, i).start()

    for sweep in range(SWEEPS):
        if sweep == 0:
            source = sources
        else:
            for direction, exists in ((0, ax_down), (1, ax_up)):

                @pl.when(exists)
                def _():
                    for a in mine + other:
                        side(direction, a).wait_recv()

            for a in range(stations):
                for c in range(cells):
                    total = sources[a, c]
                    for j, place in enumerate((0, 1, 3, 4)):
                        at = a + place
                        if at < WIDTH:
                            near = low[at, c]
                        elif at < WIDTH + stations:
                            near = field[at - WIDTH, c]
                        else:
                            near = high[at - WIDTH - stations, c]
                        k = (a * cells + c) * 4 + j
                        total = total - axial[:, k : k + 1] * near
                    line[a, c] = total
            source = line

        for i in range(half):
            sent[sweep, 0, i] = first_guess(source, other[i])
            swap(sweep, 0, i).start()
        for i in range(half):
            sent[sweep, 1, i] = first_turn(other[i])
            swap(sweep, 1, i).start()
        if sweep == 0:
            for i in range(half):
                turned, product = other_responses(other[i], kept[i])
                sent_matrix[1, i] = turned
                swap_matrix(1, i).start()
                sent_matrix[2, i] = product
                swap_matrix(2, i).start()
            for i in range(half):
                a = mine[i]
                forms(a)
                answers = inner_responses(a)
                turned, product = other_responses(a, answers)
                own_matrix[0, i] = answers[-1]
                own_matrix[1, i] = turned
                own_matrix[2, i] = product
        for i in range(half):
            local[0, i] = first_guess(source, mine[i])
            local[1, i] = first_turn(mine[i])
        if sweep == 0:
            for i in range(half):
                swap_matrix(0, i).wait_recv()
                near, far = ordered(own_matrix[0, i], got_matrix[0, i])
                keep(pair, (0, i), near)
                keep(pair, (1, i), far)
                keep(pair, (2, i), apply(pair, (1, i), near))

        up, down = 2 * sweep, 2 * sweep + 1
        for i in range(half):
            swap(sweep, 0, i).wait_recv()
            near, far = ordered(local[0, i], got[sweep, 0, i])
            whole = far + apply(pair, (1, i), near)

            @pl.when(has_down)
            def _():
                hop(up, i).wait_recv()

            incoming = arriving[up, i]

            @pl.when(has_up)
            def _():
                leaving[up, i] = whole + apply(pair, (2, i), incoming)
                hop(up, i).start()

            middle = near + apply(pair, (0, i), incoming)
            own_in, foreign_in = ordered(incoming, middle)
            local[2, i] = own_in
            sent[sweep, 2, i] = foreign_in
            swap(sweep, 2, i).start()
            if sweep == 0:
                swap_matrix(1, i).wait_recv()
                swap_matrix(2, i).wait_recv()
                near, far = ordered(own_matrix[1, i], got_matrix[1, i])
                keep(pair, (3, i), near)
                keep(pair, (4, i), far)
                near, far = ordered(own_matrix[2, i], got_matrix[2, i])
                keep(pair, (5, i), near)
                keep(pair, (6, i), far)
                keep(pair, (7, i), apply(pair, (5, i), far))
            swap(sweep, 1, i).wait_recv()
            near, far = ordered(local[1, i], got[sweep, 1, i])
            far = far + apply(pair, (4, i), middle)
            whole = near + apply(pair, (3, i), incoming) + apply(pair, (5, i), far)
            local[3, i] = far
            local[4, i] = whole

            @pl.when(top)
            def _():
                leaving[down, i] = whole
                hop(down, i).start()

        for i in range(half):
            inner_update(mine[i], local[2, i])
        for i in range(half):
            swap(sweep, 2, i).wait_recv()
            inner_update(other[i], got[sweep, 2, i])
        for i in range(half):

            @pl.when(has_up)
            def _():
                hop(down, i).wait_recv()

            incoming = arriving[down, i]

            @pl.when(jnp.logical_and(has_up, has_down))
            def _():
                leaving[down, i] = local[4, i] + apply(pair, (7, i), incoming)
                hop(down, i).start()

            middle = local[3, i] + apply(pair, (6, i), incoming)
            foreign_in, own_in = ordered(incoming, middle)
            sent[sweep, 3, i] = foreign_in
            swap(sweep, 3, i).start()
            local[2, i] = own_in

        target = field if sweep < SWEEPS - 1 else out

        def share(a):
            for direction, exists in ((0, ax_up), (1, ax_down)):

                @pl.when(exists)
                def _():
                    side(direction, a).start()

        for i in range(half):
            outer_finish(target, mine[i], local[2, i])
            if sweep < SWEEPS - 1:
                share(mine[i])
        for i in range(half):
            swap(sweep, 3, i).wait_recv()
            outer_finish(target, other[i], got[sweep, 3, i])
            if sweep < SWEEPS - 1:
                share(other[i])

    for i in range(half):
        for kind in range(3):
            swap_matrix(kind, i).wait_send()
        for sweep in range(SWEEPS):
            for kind in range(4):
                swap(sweep, kind, i).wait_send()

            @pl.when(has_up)
            def _():
                hop(2 * sweep, i).wait_send()

            @pl.when(has_down)
            def _():
                hop(2 * sweep + 1, i).wait_send()

    for direction, exists in ((0, ax_up), (1, ax_down)):

        @pl.when(exists)
        def _():
            for a in mine + other:
                side(direction, a).wait_send()


def on_device(segments, blocks, sources, block_inverse, radial_coupling, axial_coupling):
    stations, cells, species, columns = sources.shape
    half = stations // 2
    assert segments % 2 == 0 and segments >= 4 and stations == WIDTH
    axial = axial_coupling.reshape(-1, species).T
    matrix = pltpu.VMEM((stations, cells, 2, species, species), jnp.bfloat16)
    square = pltpu.VMEM((3, half, species, species), jnp.float32)
    grid = pltpu.VMEM((stations, cells, species, columns), jnp.float32)
    swaps = pltpu.VMEM((SWEEPS, 4, half, species, columns), jnp.float32)
    slots = pltpu.VMEM((2 * SWEEPS, half, species, columns), jnp.float32)
    sems = [
        pltpu.SemaphoreType.DMA(shape)
        for shape in ((3, half), (SWEEPS, 4, half), (2 * SWEEPS, half), (2, stations))
        for side in range(2)
    ]
    spec = pl.BlockSpec(memory_space=pltpu.VMEM)
    return pl.pallas_call(
        functools.partial(kernel, segments, blocks),
        out_shape=jax.ShapeDtypeStruct(sources.shape, jnp.float32),
        in_specs=[spec] * 4,
        out_specs=spec,
        scratch_shapes=[
            matrix,
            matrix,
            matrix,
            pltpu.VMEM((8, half, 2, species, species), jnp.bfloat16),
            square,
            square,
            square,
            grid,
            grid,
            grid,
            grid,
            grid,
            swaps,
            swaps,
            pltpu.VMEM((5, half, species, columns), jnp.float32),
            slots,
            slots,
            *sems,
        ],
        compiler_params=pltpu.CompilerParams(
            collective_id=0, has_side_effects=True, vmem_limit_bytes=48 << 20
        ),
    )(sources, block_inverse, radial_coupling, axial)


def solution(mesh):
    placed = P("ax", "rad", None, None)
    return jax.shard_map(
        functools.partial(on_device, mesh.shape["rad"], mesh.shape["ax"]),
        mesh=mesh,
        in_specs=(placed,) * 4,
        out_specs=placed,
        check_vma=False,
    )
```

```python
import functools
import jax
import jax.numpy as jnp
from jax import lax
from jax.experimental import pallas as pl
from jax.experimental.pallas import tpu as pltpu
from jax.sharding import PartitionSpec as P

SWEEPS = 2
WIDTH = 2
MESH = pl.DeviceIdType.MESH


def split(value):
    high = value.astype(jnp.bfloat16)
    low = (value - high.astype(jnp.float32)).astype(jnp.bfloat16)
    return high, low


def keep(ref, index, value):
    high, low = split(value)
    ref[index + (0,)] = high
    ref[index + (1,)] = low


def apply(ref, index, operand):
    high, low = split(operand)
    left_high = ref[index + (0,)]
    left_low = ref[index + (1,)]
    dot = functools.partial(jnp.dot, preferred_element_type=jnp.float32)
    return dot(left_high, high) + (dot(left_high, low) + dot(left_low, high))


def kernel(
    segments,
    blocks,
    sources,
    inverse,
    radial,
    axial,
    out,
    plain,
    inner,
    outer,
    pair,
    sent_matrix,
    got_matrix,
    own_matrix,
    fold_out,
    fold_in,
    line,
    value,
    field,
    low,
    high,
    sent,
    got,
    local,
    arriving,
    leaving,
    early_out,
    early_in,
    matrix_send,
    matrix_recv,
    pair_send,
    pair_recv,
    hop_send,
    hop_recv,
    side_send,
    side_recv,
    early_send,
    early_recv,
    fold_send,
    fold_recv,
):
    stations, cells = sources.shape[:2]
    half = stations // 2
    rad = lax.axis_index("rad")
    ax = lax.axis_index("ax")
    parity = lax.rem(rad, 2)
    is_first = parity == 0
    top, bottom = rad >= segments - 2, rad < 2
    turn = jnp.logical_and(rad >= segments - 4, rad < segments - 2)
    below = rad < segments - 4
    has_up, has_down = jnp.logical_not(top), jnp.logical_not(bottom)
    ax_up, ax_down = ax < blocks - 1, ax > 0
    partner = {"rad": rad + 1 - 2 * parity}
    mine = [parity * half + i for i in range(half)]
    other = [(1 - parity) * half + i for i in range(half)]

    barrier = pltpu.get_barrier_semaphore()
    neighbours = (
        (has_up, {"rad": rad + 2}),
        (has_down, {"rad": rad - 2}),
        (ax_up, {"ax": ax + 1}),
        (ax_down, {"ax": ax - 1}),
    )
    pl.semaphore_signal(barrier, inc=1, device_id=partner, device_id_type=MESH)
    for exists, device in neighbours:

        @pl.when(exists)
        def _():
            pl.semaphore_signal(barrier, inc=1, device_id=device, device_id_type=MESH)

    def remote(source, target, send_sem, recv_sem, device):
        return pltpu.make_async_remote_copy(
            src_ref=source,
            dst_ref=target,
            send_sem=send_sem,
            recv_sem=recv_sem,
            device_id=device,
            device_id_type=MESH,
        )

    def swap_matrix(kind, i):
        at = (kind, i)
        return remote(
            sent_matrix.at[at], got_matrix.at[at], matrix_send.at[at], matrix_recv.at[at], partner
        )

    def swap(sweep, kind, i):
        at = (sweep, kind, i)
        return remote(sent.at[at], got.at[at], pair_send.at[at], pair_recv.at[at], partner)

    def hop(number, i):
        at = (number, i)
        device = {"rad": rad + 2 if number % 2 == 0 else rad - 2}
        return remote(leaving.at[at], arriving.at[at], hop_send.at[at], hop_recv.at[at], device)

    def early(sweep, i):
        at = (sweep, i)
        device = {"rad": jnp.where(top, rad - 2, rad + 2)}
        return remote(early_out.at[at], early_in.at[at], early_send.at[at], early_recv.at[at], device)

    def fold(i):
        return remote(
            fold_out.at[i], fold_in.at[i], fold_send.at[i], fold_recv.at[i], {"rad": rad - 2}
        )

    def side(direction, station):
        at = (direction, station)
        device = {"ax": ax + 1 if direction == 0 else ax - 1}
        target = low if direction == 0 else high
        return remote(
            field.at[station], target.at[station], side_send.at[at], side_recv.at[at], device
        )

    @pl.when(bottom)
    def _():
        for number in range(0, 2 * SWEEPS, 2):
            arriving[number] = jnp.zeros(arriving.shape[1:], jnp.float32)

    @pl.when(top)
    def _():
        for number in range(1, 2 * SWEEPS, 2):
            arriving[number] = jnp.zeros(arriving.shape[1:], jnp.float32)

    @pl.when(jnp.logical_not(ax_down))
    def _():
        low[...] = jnp.zeros(low.shape, jnp.float32)

    @pl.when(jnp.logical_not(ax_up))
    def _():
        high[...] = jnp.zeros(high.shape, jnp.float32)

    def forms(a):
        for c in range(cells):
            block = inverse[a, c]
            keep(plain, (a, c), block)
            keep(inner, (a, c), block * radial[a, c, 0:1, :])
            keep(outer, (a, c), block * radial[a, c, 1:2, :])

    def inner_responses(a):
        answers = [-(inverse[a, 0] * radial[a, 0, 0:1, :])]
        for c in range(1, cells):
            answers.append(-apply(inner, (a, c), answers[-1]))
        return answers

    def other_responses(a, answers):
        turned = answers[-1]
        product = -(inverse[a, cells - 1] * radial[a, cells - 1, 1:2, :])
        for c in reversed(range(cells - 1)):
            turned = answers[c] - apply(outer, (a, c), turned)
            product = -apply(outer, (a, c), product)
        return turned, product

    def first_guess(source, a):
        previous = apply(plain, (a, 0), source[a, 0])
        value[a, 0] = previous
        for c in range(1, cells):
            previous = apply(plain, (a, c), source[a, c]) - apply(inner, (a, c), previous)
            value[a, c] = previous
        return previous

    def first_turn(a):
        following = value[a, cells - 1]
        for c in reversed(range(cells - 1)):
            following = value[a, c] - apply(outer, (a, c), following)
        return following

    def inner_update(a, incoming):
        change = -apply(inner, (a, 0), incoming)
        value[a, 0] += change
        for c in range(1, cells):
            change = -apply(inner, (a, c), change)
            value[a, c] += change

    def outer_finish(target, a, incoming):
        following = incoming
        for c in reversed(range(cells)):
            following = value[a, c] - apply(outer, (a, c), following)
            target[a, c] = following

    def ordered(own, foreign):
        return jnp.where(is_first, own, foreign), jnp.where(is_first, foreign, own)

    for i in range(half):
        forms(other[i])
    kept = [inner_responses(other[i]) for i in range(half)]
    for i in range(half):
        sent_matrix[0, i] = kept[i][-1]
    peers = 1 + sum(jnp.where(exists, 1, 0) for exists, device in neighbours)
    pl.semaphore_wait(barrier, peers)
    for i in range(half):
        swap_matrix(0, i).start()

    for sweep in range(SWEEPS):
        if sweep == 0:
            source = sources
        else:
            for direction, exists in ((0, ax_down), (1, ax_up)):

                @pl.when(exists)
                def _():
                    for a in mine + other:
                        side(direction, a).wait_recv()

            for a in range(stations):
                for c in range(cells):
                    total = sources[a, c]
                    for j, place in enumerate((0, 1, 3, 4)):
                        at = a + place
                        if at < WIDTH:
                            near = low[at, c]
                        elif at < WIDTH + stations:
                            near = field[at - WIDTH, c]
                        else:
                            near = high[at - WIDTH - stations, c]
                        k = (a * cells + c) * 4 + j
                        total = total - axial[:, k : k + 1] * near
                    line[a, c] = total
            source = line

        for i in range(half):
            sent[sweep, 0, i] = first_guess(source, other[i])
            swap(sweep, 0, i).start()
        for i in range(half):
            sent[sweep, 1, i] = first_turn(other[i])
            swap(sweep, 1, i).start()
        if sweep == 0:
            for i in range(half):
                turned, product = other_responses(other[i], kept[i])
                sent_matrix[1, i] = turned
                swap_matrix(1, i).start()
                sent_matrix[2, i] = product
                swap_matrix(2, i).start()
            for i in range(half):
                a = mine[i]
                forms(a)
                answers = inner_responses(a)
                turned, product = other_responses(a, answers)
                own_matrix[0, i] = answers[-1]
                own_matrix[1, i] = turned
                own_matrix[2, i] = product
        for i in range(half):
            local[0, i] = first_guess(source, mine[i])
            local[1, i] = first_turn(mine[i])
        if sweep == 0:
            for i in range(half):
                swap_matrix(0, i).wait_recv()
                near, far = ordered(own_matrix[0, i], got_matrix[0, i])
                keep(pair, (0, i), near)
                keep(pair, (1, i), far)

        up, down = 2 * sweep, 2 * sweep + 1

        def late_forms(i):
            swap_matrix(1, i).wait_recv()
            swap_matrix(2, i).wait_recv()
            near, far = ordered(own_matrix[1, i], got_matrix[1, i])
            keep(pair, (3, i), near)
            keep(pair, (4, i), far)
            near, far = ordered(own_matrix[2, i], got_matrix[2, i])
            keep(pair, (5, i), near)
            keep(pair, (6, i), far)
            keep(pair, (7, i), apply(pair, (5, i), far))

        def whole_response(i):
            first, _ = ordered(own_matrix[0, i], got_matrix[0, i])
            turned, _ = ordered(own_matrix[1, i], got_matrix[1, i])
            return turned + apply(pair, (5, i), apply(pair, (4, i), first))

        for i in range(half):
            swap(sweep, 0, i).wait_recv()
            near, far = ordered(local[0, i], got[sweep, 0, i])
            whole = far + apply(pair, (1, i), near)

            @pl.when(turn)
            def _():
                early_out[sweep, i] = whole
                early(sweep, i).start()

            @pl.when(bottom)
            def _():
                leaving[up, i] = whole
                hop(up, i).start()

            if sweep == 0:
                first, _ = ordered(own_matrix[0, i], got_matrix[0, i])
                product = apply(pair, (1, i), first)
                fold_out[i] = product
                keep(pair, (2, i), product)

                @pl.when(top)
                def _():
                    late_forms(i)
                    response = whole_response(i)
                    fold_out[i] = response
                    fold(i).start()
                    keep(pair, (8, i), response)

                @pl.when(turn)
                def _():
                    late_forms(i)
                    response = whole_response(i)
                    fold(i).wait_recv()
                    keep(pair, (9, i), fold_in[i])
                    beyond = apply(pair, (9, i), fold_out[i])
                    keep(pair, (8, i), beyond)
                    keep(pair, (9, i), response + apply(pair, (7, i), beyond))

            swap(sweep, 1, i).wait_recv()
            near_turn, far_turn = ordered(local[1, i], got[sweep, 1, i])

            def unfed():
                return near_turn + apply(pair, (5, i), far_turn + apply(pair, (4, i), near))

            @pl.when(top)
            def _():
                guess = unfed()
                early(sweep, i).wait_recv()
                early_out[sweep, i] = guess + apply(pair, (8, i), early_in[sweep, i])
                early(sweep, i).start()

            @pl.when(turn)
            def _():
                guess = unfed()
                early(sweep, i).wait_recv()
                local[4, i] = guess + apply(pair, (7, i), early_in[sweep, i])

            @pl.when(has_down)
            def _():
                hop(up, i).wait_recv()

            incoming = arriving[up, i]

            @pl.when(turn)
            def _():
                leaving[down, i] = local[4, i] + apply(pair, (9, i), incoming)
                hop(down, i).start()

            @pl.when(jnp.logical_and(has_up, has_down))
            def _():
                leaving[up, i] = whole + apply(pair, (2, i), incoming)
                hop(up, i).start()

            @pl.when(turn)
            def _():
                arriving[down, i] = early_in[sweep, i] + apply(pair, (8, i), incoming)

            middle = near + apply(pair, (0, i), incoming)
            own_in, foreign_in = ordered(incoming, middle)
            local[2, i] = own_in
            sent[sweep, 2, i] = foreign_in
            swap(sweep, 2, i).start()
            if sweep == 0:

                @pl.when(below)
                def _():
                    late_forms(i)

            far = far_turn + apply(pair, (4, i), middle)
            local[3, i] = far

            @pl.when(below)
            def _():
                local[4, i] = near_turn + apply(pair, (3, i), incoming) + apply(pair, (5, i), far)

        for i in range(half):
            inner_update(mine[i], local[2, i])
        for i in range(half):
            swap(sweep, 2, i).wait_recv()
            inner_update(other[i], got[sweep, 2, i])
        for i in range(half):

            @pl.when(below)
            def _():
                hop(down, i).wait_recv()

            incoming = arriving[down, i]

            @pl.when(jnp.logical_and(below, has_down))
            def _():
                leaving[down, i] = local[4, i] + apply(pair, (7, i), incoming)
                hop(down, i).start()

            middle = local[3, i] + apply(pair, (6, i), incoming)
            foreign_in, own_in = ordered(incoming, middle)
            sent[sweep, 3, i] = foreign_in
            swap(sweep, 3, i).start()
            local[2, i] = own_in

        target = field if sweep < SWEEPS - 1 else out

        def share(a):
            for direction, exists in ((0, ax_up), (1, ax_down)):

                @pl.when(exists)
                def _():
                    side(direction, a).start()

        for i in range(half):
            outer_finish(target, mine[i], local[2, i])
            if sweep < SWEEPS - 1:
                share(mine[i])
        for i in range(half):
            swap(sweep, 3, i).wait_recv()
            outer_finish(target, other[i], got[sweep, 3, i])
            if sweep < SWEEPS - 1:
                share(other[i])

    for i in range(half):
        for kind in range(3):
            swap_matrix(kind, i).wait_send()
        for sweep in range(SWEEPS):
            for kind in range(4):
                swap(sweep, kind, i).wait_send()

            @pl.when(has_up)
            def _():
                hop(2 * sweep, i).wait_send()

            @pl.when(jnp.logical_and(has_up, has_down))
            def _():
                hop(2 * sweep + 1, i).wait_send()

            @pl.when(jnp.logical_not(below))
            def _():
                early(sweep, i).wait_send()

        @pl.when(top)
        def _():
            fold(i).wait_send()

    for direction, exists in ((0, ax_up), (1, ax_down)):

        @pl.when(exists)
        def _():
            for a in mine + other:
                side(direction, a).wait_send()


def on_device(segments, blocks, sources, block_inverse, radial_coupling, axial_coupling):
    stations, cells, species, columns = sources.shape
    half = stations // 2
    assert segments % 2 == 0 and segments >= 6 and stations == WIDTH
    axial = axial_coupling.reshape(-1, species).T
    matrix = pltpu.VMEM((stations, cells, 2, species, species), jnp.bfloat16)
    square = pltpu.VMEM((3, half, species, species), jnp.float32)
    grid = pltpu.VMEM((stations, cells, species, columns), jnp.float32)
    swaps = pltpu.VMEM((SWEEPS, 4, half, species, columns), jnp.float32)
    slots = pltpu.VMEM((2 * SWEEPS, half, species, columns), jnp.float32)
    earlies = pltpu.VMEM((SWEEPS, half, species, columns), jnp.float32)
    fold = pltpu.VMEM((half, species, species), jnp.float32)
    sems = [
        pltpu.SemaphoreType.DMA(shape)
        for shape in ((3, half), (SWEEPS, 4, half), (2 * SWEEPS, half), (2, stations), (SWEEPS, half), (half,))
        for side in range(2)
    ]
    spec = pl.BlockSpec(memory_space=pltpu.VMEM)
    return pl.pallas_call(
        functools.partial(kernel, segments, blocks),
        out_shape=jax.ShapeDtypeStruct(sources.shape, jnp.float32),
        in_specs=[spec] * 4,
        out_specs=spec,
        scratch_shapes=[
            matrix,
            matrix,
            matrix,
            pltpu.VMEM((10, half, 2, species, species), jnp.bfloat16),
            square,
            square,
            square,
            fold,
            fold,
            grid,
            grid,
            grid,
            grid,
            grid,
            swaps,
            swaps,
            pltpu.VMEM((5, half, species, columns), jnp.float32),
            slots,
            slots,
            earlies,
            earlies,
            *sems,
        ],
        compiler_params=pltpu.CompilerParams(
            collective_id=0, has_side_effects=True, vmem_limit_bytes=48 << 20
        ),
    )(sources, block_inverse, radial_coupling, axial)


def solution(mesh):
    placed = P("ax", "rad", None, None)
    return jax.shard_map(
        functools.partial(on_device, mesh.shape["rad"], mesh.shape["ax"]),
        mesh=mesh,
        in_specs=(placed,) * 4,
        out_specs=placed,
        check_vma=False,
    )
```

```python
import functools
import jax
import jax.numpy as jnp
from jax import lax
from jax.experimental import pallas as pl
from jax.experimental.pallas import tpu as pltpu
from jax.sharding import PartitionSpec as P

SWEEPS = 2
WIDTH = 2
MESH = pl.DeviceIdType.MESH


def split(value):
    high = value.astype(jnp.bfloat16)
    low = (value - high.astype(jnp.float32)).astype(jnp.bfloat16)
    return high, low


def keep(ref, index, value):
    high, low = split(value)
    ref[index + (0,)] = high
    ref[index + (1,)] = low


def apply(ref, index, operand):
    high, low = split(operand)
    left_high = ref[index + (0,)]
    left_low = ref[index + (1,)]
    dot = functools.partial(jnp.dot, preferred_element_type=jnp.float32)
    return dot(left_high, high) + (dot(left_high, low) + dot(left_low, high))


def kernel(
    segments,
    blocks,
    sources,
    inverse,
    radial,
    axial,
    out,
    plain,
    inner,
    outer,
    pair,
    far_inner,
    far_outer,
    got_block,
    got_radial,
    got_matrix,
    own_matrix,
    fold_out,
    fold_in,
    line,
    value,
    field,
    low,
    high,
    sent,
    got,
    local,
    arriving,
    leaving,
    early_out,
    early_in,
    matrix_send,
    matrix_recv,
    pair_send,
    pair_recv,
    hop_send,
    hop_recv,
    side_send,
    side_recv,
    early_send,
    early_recv,
    fold_send,
    fold_recv,
):
    stations, cells = sources.shape[:2]
    half = stations // 2
    rad = lax.axis_index("rad")
    ax = lax.axis_index("ax")
    parity = lax.rem(rad, 2)
    is_first = parity == 0
    top, bottom = rad >= segments - 2, rad < 2
    turn = jnp.logical_and(rad >= segments - 4, rad < segments - 2)
    below = rad < segments - 4
    has_up, has_down = jnp.logical_not(top), jnp.logical_not(bottom)
    ax_up, ax_down = ax < blocks - 1, ax > 0
    partner = {"rad": rad + 1 - 2 * parity}
    mine = [parity * half + i for i in range(half)]
    other = [(1 - parity) * half + i for i in range(half)]

    barrier = pltpu.get_barrier_semaphore()
    neighbours = (
        (has_up, {"rad": rad + 2}),
        (has_down, {"rad": rad - 2}),
        (ax_up, {"ax": ax + 1}),
        (ax_down, {"ax": ax - 1}),
    )
    pl.semaphore_signal(barrier, inc=1, device_id=partner, device_id_type=MESH)
    for exists, device in neighbours:

        @pl.when(exists)
        def _():
            pl.semaphore_signal(barrier, inc=1, device_id=device, device_id_type=MESH)

    def remote(source, target, send_sem, recv_sem, device):
        return pltpu.make_async_remote_copy(
            src_ref=source,
            dst_ref=target,
            send_sem=send_sem,
            recv_sem=recv_sem,
            device_id=device,
            device_id_type=MESH,
        )

    def swap_block(i, c):
        at = (c, i)
        source = inverse.at[other[i], c]
        return remote(source, got_block.at[i, c], matrix_send.at[at], matrix_recv.at[at], partner)

    def swap_radial(i):
        at = (cells, i)
        source = radial.at[other[i]]
        return remote(source, got_radial.at[i], matrix_send.at[at], matrix_recv.at[at], partner)

    def swap(sweep, kind, i):
        at = (sweep, kind, i)
        return remote(sent.at[at], got.at[at], pair_send.at[at], pair_recv.at[at], partner)

    def hop(number, i):
        at = (number, i)
        device = {"rad": rad + 2 if number % 2 == 0 else rad - 2}
        return remote(leaving.at[at], arriving.at[at], hop_send.at[at], hop_recv.at[at], device)

    def early(sweep, i):
        at = (sweep, i)
        device = {"rad": jnp.where(top, rad - 2, rad + 2)}
        return remote(early_out.at[at], early_in.at[at], early_send.at[at], early_recv.at[at], device)

    def fold(i):
        return remote(
            fold_out.at[i], fold_in.at[i], fold_send.at[i], fold_recv.at[i], {"rad": rad - 2}
        )

    def side(direction, station):
        at = (direction, station)
        device = {"ax": ax + 1 if direction == 0 else ax - 1}
        target = low if direction == 0 else high
        return remote(
            field.at[station], target.at[station], side_send.at[at], side_recv.at[at], device
        )

    @pl.when(bottom)
    def _():
        for number in range(0, 2 * SWEEPS, 2):
            arriving[number] = jnp.zeros(arriving.shape[1:], jnp.float32)

    @pl.when(top)
    def _():
        for number in range(1, 2 * SWEEPS, 2):
            arriving[number] = jnp.zeros(arriving.shape[1:], jnp.float32)

    @pl.when(jnp.logical_not(ax_down))
    def _():
        low[...] = jnp.zeros(low.shape, jnp.float32)

    @pl.when(jnp.logical_not(ax_up))
    def _():
        high[...] = jnp.zeros(high.shape, jnp.float32)

    def forms(a):
        for c in range(cells):
            block = inverse[a, c]
            keep(plain, (a, c), block)
            keep(inner, (a, c), block * radial[a, c, 0:1, :])
            keep(outer, (a, c), block * radial[a, c, 1:2, :])

    def responses(target, i, block, rates, inner, outer, a):
        answers = [-(block[a, 0] * rates[a, 0, 0:1, :])]
        for c in range(1, cells):
            answers.append(-apply(inner, (a, c), answers[-1]))
        turned = answers[-1]
        product = -(block[a, cells - 1] * rates[a, cells - 1, 1:2, :])
        for c in reversed(range(cells - 1)):
            turned = answers[c] - apply(outer, (a, c), turned)
            product = -apply(outer, (a, c), product)
        target[0, i] = answers[-1]
        target[1, i] = turned
        target[2, i] = product

    def first_guess(source, a):
        previous = apply(plain, (a, 0), source[a, 0])
        value[a, 0] = previous
        for c in range(1, cells):
            previous = apply(plain, (a, c), source[a, c]) - apply(inner, (a, c), previous)
            value[a, c] = previous
        return previous

    def first_turn(a):
        following = value[a, cells - 1]
        for c in reversed(range(cells - 1)):
            following = value[a, c] - apply(outer, (a, c), following)
        return following

    def inner_update(a, incoming):
        change = -apply(inner, (a, 0), incoming)
        value[a, 0] += change
        for c in range(1, cells):
            change = -apply(inner, (a, c), change)
            value[a, c] += change

    def outer_finish(target, a, incoming):
        following = incoming
        for c in reversed(range(cells)):
            following = value[a, c] - apply(outer, (a, c), following)
            target[a, c] = following

    def ordered(own, foreign):
        return jnp.where(is_first, own, foreign), jnp.where(is_first, foreign, own)

    peers = 1 + sum(jnp.where(exists, 1, 0) for exists, device in neighbours)
    pl.semaphore_wait(barrier, peers)
    for i in range(half):
        swap_radial(i).start()
        for c in range(cells):
            swap_block(i, c).start()
    for i in range(half):
        forms(other[i])

    for sweep in range(SWEEPS):
        if sweep == 0:
            source = sources
        else:
            for direction, exists in ((0, ax_down), (1, ax_up)):

                @pl.when(exists)
                def _():
                    for a in mine + other:
                        side(direction, a).wait_recv()

            for a in range(stations):
                for c in range(cells):
                    total = sources[a, c]
                    for j, place in enumerate((0, 1, 3, 4)):
                        at = a + place
                        if at < WIDTH:
                            near = low[at, c]
                        elif at < WIDTH + stations:
                            near = field[at - WIDTH, c]
                        else:
                            near = high[at - WIDTH - stations, c]
                        k = (a * cells + c) * 4 + j
                        total = total - axial[:, k : k + 1] * near
                    line[a, c] = total
            source = line

        for i in range(half):
            sent[sweep, 0, i] = first_guess(source, other[i])
            swap(sweep, 0, i).start()
        for i in range(half):
            sent[sweep, 1, i] = first_turn(other[i])
            swap(sweep, 1, i).start()
        if sweep == 0:
            for i in range(half):
                forms(mine[i])
                responses(own_matrix, i, inverse, radial, inner, outer, mine[i])
        for i in range(half):
            local[0, i] = first_guess(source, mine[i])
            local[1, i] = first_turn(mine[i])
        if sweep == 0:
            for i in range(half):
                swap_radial(i).wait_recv()
                for c in range(cells):
                    swap_block(i, c).wait_recv()
                    block = got_block[i, c]
                    keep(far_inner, (i, c), block * got_radial[i, c, 0:1, :])
                    keep(far_outer, (i, c), block * got_radial[i, c, 1:2, :])
                responses(got_matrix, i, got_block, got_radial, far_inner, far_outer, i)
                near, far = ordered(own_matrix[0, i], got_matrix[0, i])
                keep(pair, (0, i), near)
                keep(pair, (1, i), far)

        up, down = 2 * sweep, 2 * sweep + 1

        def late_forms(i):
            near, far = ordered(own_matrix[1, i], got_matrix[1, i])
            keep(pair, (3, i), near)
            keep(pair, (4, i), far)
            near, far = ordered(own_matrix[2, i], got_matrix[2, i])
            keep(pair, (5, i), near)
            keep(pair, (6, i), far)
            keep(pair, (7, i), apply(pair, (5, i), far))

        def whole_response(i):
            first, _ = ordered(own_matrix[0, i], got_matrix[0, i])
            turned, _ = ordered(own_matrix[1, i], got_matrix[1, i])
            return turned + apply(pair, (5, i), apply(pair, (4, i), first))

        for i in range(half):
            swap(sweep, 0, i).wait_recv()
            near, far = ordered(local[0, i], got[sweep, 0, i])
            whole = far + apply(pair, (1, i), near)

            @pl.when(turn)
            def _():
                early_out[sweep, i] = whole
                early(sweep, i).start()

            @pl.when(bottom)
            def _():
                leaving[up, i] = whole
                hop(up, i).start()

            if sweep == 0:
                first, _ = ordered(own_matrix[0, i], got_matrix[0, i])
                product = apply(pair, (1, i), first)
                fold_out[i] = product
                keep(pair, (2, i), product)

                @pl.when(top)
                def _():
                    late_forms(i)
                    response = whole_response(i)
                    fold_out[i] = response
                    fold(i).start()
                    keep(pair, (8, i), response)

                @pl.when(turn)
                def _():
                    late_forms(i)
                    response = whole_response(i)
                    fold(i).wait_recv()
                    keep(pair, (9, i), fold_in[i])
                    beyond = apply(pair, (9, i), fold_out[i])
                    keep(pair, (8, i), beyond)
                    keep(pair, (9, i), response + apply(pair, (7, i), beyond))

            swap(sweep, 1, i).wait_recv()
            near_turn, far_turn = ordered(local[1, i], got[sweep, 1, i])

            def unfed():
                return near_turn + apply(pair, (5, i), far_turn + apply(pair, (4, i), near))

            @pl.when(top)
            def _():
                guess = unfed()
                early(sweep, i).wait_recv()
                early_out[sweep, i] = guess + apply(pair, (8, i), early_in[sweep, i])
                early(sweep, i).start()

            @pl.when(turn)
            def _():
                guess = unfed()
                early(sweep, i).wait_recv()
                local[4, i] = guess + apply(pair, (7, i), early_in[sweep, i])

            @pl.when(has_down)
            def _():
                hop(up, i).wait_recv()

            incoming = arriving[up, i]

            @pl.when(turn)
            def _():
                leaving[down, i] = local[4, i] + apply(pair, (9, i), incoming)
                hop(down, i).start()

            @pl.when(jnp.logical_and(has_up, has_down))
            def _():
                leaving[up, i] = whole + apply(pair, (2, i), incoming)
                hop(up, i).start()

            @pl.when(turn)
            def _():
                arriving[down, i] = early_in[sweep, i] + apply(pair, (8, i), incoming)

            middle = near + apply(pair, (0, i), incoming)
            own_in, foreign_in = ordered(incoming, middle)
            local[2, i] = own_in
            sent[sweep, 2, i] = foreign_in
            swap(sweep, 2, i).start()
            if sweep == 0:

                @pl.when(below)
                def _():
                    late_forms(i)

            far = far_turn + apply(pair, (4, i), middle)
            local[3, i] = far

            @pl.when(below)
            def _():
                local[4, i] = near_turn + apply(pair, (3, i), incoming) + apply(pair, (5, i), far)

        for i in range(half):
            inner_update(mine[i], local[2, i])
        for i in range(half):
            swap(sweep, 2, i).wait_recv()
            inner_update(other[i], got[sweep, 2, i])
        for i in range(half):

            @pl.when(below)
            def _():
                hop(down, i).wait_recv()

            incoming = arriving[down, i]

            @pl.when(jnp.logical_and(below, has_down))
            def _():
                leaving[down, i] = local[4, i] + apply(pair, (7, i), incoming)
                hop(down, i).start()

            middle = local[3, i] + apply(pair, (6, i), incoming)
            foreign_in, own_in = ordered(incoming, middle)
            sent[sweep, 3, i] = foreign_in
            swap(sweep, 3, i).start()
            local[2, i] = own_in

        target = field if sweep < SWEEPS - 1 else out

        def share(a):
            for direction, exists in ((0, ax_up), (1, ax_down)):

                @pl.when(exists)
                def _():
                    side(direction, a).start()

        for i in range(half):
            outer_finish(target, mine[i], local[2, i])
            if sweep < SWEEPS - 1:
                share(mine[i])
        for i in range(half):
            swap(sweep, 3, i).wait_recv()
            outer_finish(target, other[i], got[sweep, 3, i])
            if sweep < SWEEPS - 1:
                share(other[i])

    for i in range(half):
        swap_radial(i).wait_send()
        for c in range(cells):
            swap_block(i, c).wait_send()
        for sweep in range(SWEEPS):
            for kind in range(4):
                swap(sweep, kind, i).wait_send()

            @pl.when(has_up)
            def _():
                hop(2 * sweep, i).wait_send()

            @pl.when(jnp.logical_and(has_up, has_down))
            def _():
                hop(2 * sweep + 1, i).wait_send()

            @pl.when(jnp.logical_not(below))
            def _():
                early(sweep, i).wait_send()

        @pl.when(top)
        def _():
            fold(i).wait_send()

    for direction, exists in ((0, ax_up), (1, ax_down)):

        @pl.when(exists)
        def _():
            for a in mine + other:
                side(direction, a).wait_send()


def on_device(segments, blocks, sources, block_inverse, radial_coupling, axial_coupling):
    stations, cells, species, columns = sources.shape
    half = stations // 2
    assert segments % 2 == 0 and segments >= 6 and stations == WIDTH
    axial = axial_coupling.reshape(-1, species).T
    matrix = pltpu.VMEM((stations, cells, 2, species, species), jnp.bfloat16)
    far_matrix = pltpu.VMEM((half, cells, 2, species, species), jnp.bfloat16)
    square = pltpu.VMEM((3, half, species, species), jnp.float32)
    grid = pltpu.VMEM((stations, cells, species, columns), jnp.float32)
    swaps = pltpu.VMEM((SWEEPS, 4, half, species, columns), jnp.float32)
    slots = pltpu.VMEM((2 * SWEEPS, half, species, columns), jnp.float32)
    earlies = pltpu.VMEM((SWEEPS, half, species, columns), jnp.float32)
    fold = pltpu.VMEM((half, species, species), jnp.float32)
    sems = [
        pltpu.SemaphoreType.DMA(shape)
        for shape in ((cells + 1, half), (SWEEPS, 4, half), (2 * SWEEPS, half), (2, stations), (SWEEPS, half), (half,))
        for side in range(2)
    ]
    spec = pl.BlockSpec(memory_space=pltpu.VMEM)
    return pl.pallas_call(
        functools.partial(kernel, segments, blocks),
        out_shape=jax.ShapeDtypeStruct(sources.shape, jnp.float32),
        in_specs=[spec] * 4,
        out_specs=spec,
        scratch_shapes=[
            matrix,
            matrix,
            matrix,
            pltpu.VMEM((10, half, 2, species, species), jnp.bfloat16),
            far_matrix,
            far_matrix,
            pltpu.VMEM((half, cells, species, species), jnp.float32),
            pltpu.VMEM((half, *radial_coupling.shape[1:]), jnp.float32),
            square,
            square,
            fold,
            fold,
            grid,
            grid,
            grid,
            grid,
            grid,
            swaps,
            swaps,
            pltpu.VMEM((5, half, species, columns), jnp.float32),
            slots,
            slots,
            earlies,
            earlies,
            *sems,
        ],
        compiler_params=pltpu.CompilerParams(
            collective_id=0, has_side_effects=True, vmem_limit_bytes=48 << 20
        ),
    )(sources, block_inverse, radial_coupling, axial)


def solution(mesh):
    placed = P("ax", "rad", None, None)
    return jax.shard_map(
        functools.partial(on_device, mesh.shape["rad"], mesh.shape["ax"]),
        mesh=mesh,
        in_specs=(placed,) * 4,
        out_specs=placed,
        check_vma=False,
    )
```

```python
import functools
import jax
import jax.numpy as jnp
from jax import lax
from jax.experimental import pallas as pl
from jax.experimental.pallas import tpu as pltpu
from jax.sharding import PartitionSpec as P

SWEEPS = 2
WIDTH = 2
MESH = pl.DeviceIdType.MESH


def split(value):
    high = value.astype(jnp.bfloat16)
    low = (value - high.astype(jnp.float32)).astype(jnp.bfloat16)
    return high, low


def keep(ref, index, value):
    high, low = split(value)
    ref[index + (0,)] = high
    ref[index + (1,)] = low


def apply(ref, index, operand):
    high, low = split(operand)
    left_high = ref[index + (0,)]
    left_low = ref[index + (1,)]
    dot = functools.partial(jnp.dot, preferred_element_type=jnp.float32)
    return dot(left_high, high) + (dot(left_high, low) + dot(left_low, high))


def kernel(
    segments,
    blocks,
    given_sources,
    given_inverse,
    radial,
    axial,
    out,
    sources,
    inverse,
    plain,
    inner,
    outer,
    pair,
    far_inner,
    far_outer,
    got_block,
    got_radial,
    got_matrix,
    own_matrix,
    fold_out,
    fold_in,
    line,
    value,
    field,
    low,
    high,
    sent,
    got,
    local,
    arriving,
    leaving,
    early_out,
    early_in,
    matrix_send,
    matrix_recv,
    pair_send,
    pair_recv,
    hop_send,
    hop_recv,
    side_send,
    side_recv,
    early_send,
    early_recv,
    fold_send,
    fold_recv,
    load_sem,
):
    loads = (
        pltpu.make_async_copy(given_inverse, inverse, load_sem.at[0]),
        pltpu.make_async_copy(given_sources, sources, load_sem.at[1]),
    )
    for load in loads:
        load.start()
    stations, cells = sources.shape[:2]
    half = stations // 2
    rad = lax.axis_index("rad")
    ax = lax.axis_index("ax")
    parity = lax.rem(rad, 2)
    is_first = parity == 0
    top, bottom = rad >= segments - 2, rad < 2
    turn = jnp.logical_and(rad >= segments - 4, rad < segments - 2)
    below = rad < segments - 4
    has_up, has_down = jnp.logical_not(top), jnp.logical_not(bottom)
    ax_up, ax_down = ax < blocks - 1, ax > 0
    partner = {"rad": rad + 1 - 2 * parity}
    mine = [parity * half + i for i in range(half)]
    other = [(1 - parity) * half + i for i in range(half)]

    barrier = pltpu.get_barrier_semaphore()
    neighbours = (
        (has_up, {"rad": rad + 2}),
        (has_down, {"rad": rad - 2}),
        (ax_up, {"ax": ax + 1}),
        (ax_down, {"ax": ax - 1}),
    )
    pl.semaphore_signal(barrier, inc=1, device_id=partner, device_id_type=MESH)
    for exists, device in neighbours:

        @pl.when(exists)
        def _():
            pl.semaphore_signal(barrier, inc=1, device_id=device, device_id_type=MESH)

    def remote(source, target, send_sem, recv_sem, device):
        return pltpu.make_async_remote_copy(
            src_ref=source,
            dst_ref=target,
            send_sem=send_sem,
            recv_sem=recv_sem,
            device_id=device,
            device_id_type=MESH,
        )

    def swap_block(i, c):
        at = (c, i)
        source = given_inverse.at[other[i], c]
        return remote(source, got_block.at[i, c], matrix_send.at[at], matrix_recv.at[at], partner)

    def swap_radial(i):
        at = (cells, i)
        source = radial.at[other[i]]
        return remote(source, got_radial.at[i], matrix_send.at[at], matrix_recv.at[at], partner)

    def swap(sweep, kind, i):
        at = (sweep, kind, i)
        return remote(sent.at[at], got.at[at], pair_send.at[at], pair_recv.at[at], partner)

    def hop(number, i):
        at = (number, i)
        device = {"rad": rad + 2 if number % 2 == 0 else rad - 2}
        return remote(leaving.at[at], arriving.at[at], hop_send.at[at], hop_recv.at[at], device)

    def early(sweep, i):
        at = (sweep, i)
        device = {"rad": jnp.where(top, rad - 2, rad + 2)}
        return remote(early_out.at[at], early_in.at[at], early_send.at[at], early_recv.at[at], device)

    def fold(i):
        return remote(
            fold_out.at[i], fold_in.at[i], fold_send.at[i], fold_recv.at[i], {"rad": rad - 2}
        )

    def side(direction, station):
        at = (direction, station)
        device = {"ax": ax + 1 if direction == 0 else ax - 1}
        target = low if direction == 0 else high
        return remote(
            field.at[station], target.at[station], side_send.at[at], side_recv.at[at], device
        )

    @pl.when(bottom)
    def _():
        for number in range(0, 2 * SWEEPS, 2):
            arriving[number] = jnp.zeros(arriving.shape[1:], jnp.float32)

    @pl.when(top)
    def _():
        for number in range(1, 2 * SWEEPS, 2):
            arriving[number] = jnp.zeros(arriving.shape[1:], jnp.float32)

    @pl.when(jnp.logical_not(ax_down))
    def _():
        low[...] = jnp.zeros(low.shape, jnp.float32)

    @pl.when(jnp.logical_not(ax_up))
    def _():
        high[...] = jnp.zeros(high.shape, jnp.float32)

    def forms(a):
        for c in range(cells):
            block = inverse[a, c]
            keep(plain, (a, c), block)
            keep(inner, (a, c), block * radial[a, c, 0:1, :])
            keep(outer, (a, c), block * radial[a, c, 1:2, :])

    def responses(target, i, block, rates, inner, outer, a):
        answers = [-(block[a, 0] * rates[a, 0, 0:1, :])]
        for c in range(1, cells):
            answers.append(-apply(inner, (a, c), answers[-1]))
        turned = answers[-1]
        product = -(block[a, cells - 1] * rates[a, cells - 1, 1:2, :])
        for c in reversed(range(cells - 1)):
            turned = answers[c] - apply(outer, (a, c), turned)
            product = -apply(outer, (a, c), product)
        target[0, i] = answers[-1]
        target[1, i] = turned
        target[2, i] = product

    def first_guess(source, a):
        previous = apply(plain, (a, 0), source[a, 0])
        value[a, 0] = previous
        for c in range(1, cells):
            previous = apply(plain, (a, c), source[a, c]) - apply(inner, (a, c), previous)
            value[a, c] = previous
        return previous

    def first_turn(a):
        following = value[a, cells - 1]
        for c in reversed(range(cells - 1)):
            following = value[a, c] - apply(outer, (a, c), following)
        return following

    def inner_update(a, incoming):
        change = -apply(inner, (a, 0), incoming)
        value[a, 0] += change
        for c in range(1, cells):
            change = -apply(inner, (a, c), change)
            value[a, c] += change

    def outer_finish(target, a, incoming):
        following = incoming
        for c in reversed(range(cells)):
            following = value[a, c] - apply(outer, (a, c), following)
            target[a, c] = following

    def ordered(own, foreign):
        return jnp.where(is_first, own, foreign), jnp.where(is_first, foreign, own)

    peers = 1 + sum(jnp.where(exists, 1, 0) for exists, device in neighbours)
    pl.semaphore_wait(barrier, peers)
    for i in range(half):
        swap_radial(i).start()
        for c in range(cells):
            swap_block(i, c).start()
    for load in loads:
        load.wait()
    for i in range(half):
        forms(other[i])

    for sweep in range(SWEEPS):
        if sweep == 0:
            source = sources
        else:
            for direction, exists in ((0, ax_down), (1, ax_up)):

                @pl.when(exists)
                def _():
                    for a in mine + other:
                        side(direction, a).wait_recv()

            for a in range(stations):
                for c in range(cells):
                    total = sources[a, c]
                    for j, place in enumerate((0, 1, 3, 4)):
                        at = a + place
                        if at < WIDTH:
                            near = low[at, c]
                        elif at < WIDTH + stations:
                            near = field[at - WIDTH, c]
                        else:
                            near = high[at - WIDTH - stations, c]
                        k = (a * cells + c) * 4 + j
                        total = total - axial[:, k : k + 1] * near
                    line[a, c] = total
            source = line

        for i in range(half):
            sent[sweep, 0, i] = first_guess(source, other[i])
            swap(sweep, 0, i).start()
        for i in range(half):
            sent[sweep, 1, i] = first_turn(other[i])
            swap(sweep, 1, i).start()
        if sweep == 0:
            for i in range(half):
                forms(mine[i])
                responses(own_matrix, i, inverse, radial, inner, outer, mine[i])
        for i in range(half):
            local[0, i] = first_guess(source, mine[i])
            local[1, i] = first_turn(mine[i])
        if sweep == 0:
            for i in range(half):
                swap_radial(i).wait_recv()
                for c in range(cells):
                    swap_block(i, c).wait_recv()
                    block = got_block[i, c]
                    keep(far_inner, (i, c), block * got_radial[i, c, 0:1, :])
                    keep(far_outer, (i, c), block * got_radial[i, c, 1:2, :])
                responses(got_matrix, i, got_block, got_radial, far_inner, far_outer, i)
                near, far = ordered(own_matrix[0, i], got_matrix[0, i])
                keep(pair, (0, i), near)
                keep(pair, (1, i), far)

        up, down = 2 * sweep, 2 * sweep + 1

        def late_forms(i):
            near, far = ordered(own_matrix[1, i], got_matrix[1, i])
            keep(pair, (3, i), near)
            keep(pair, (4, i), far)
            near, far = ordered(own_matrix[2, i], got_matrix[2, i])
            keep(pair, (5, i), near)
            keep(pair, (6, i), far)
            keep(pair, (7, i), apply(pair, (5, i), far))

        def whole_response(i):
            first, _ = ordered(own_matrix[0, i], got_matrix[0, i])
            turned, _ = ordered(own_matrix[1, i], got_matrix[1, i])
            return turned + apply(pair, (5, i), apply(pair, (4, i), first))

        for i in range(half):
            swap(sweep, 0, i).wait_recv()
            near, far = ordered(local[0, i], got[sweep, 0, i])
            whole = far + apply(pair, (1, i), near)

            @pl.when(turn)
            def _():
                early_out[sweep, i] = whole
                early(sweep, i).start()

            @pl.when(bottom)
            def _():
                leaving[up, i] = whole
                hop(up, i).start()

            if sweep == 0:
                first, _ = ordered(own_matrix[0, i], got_matrix[0, i])
                product = apply(pair, (1, i), first)
                fold_out[i] = product
                keep(pair, (2, i), product)

                @pl.when(top)
                def _():
                    late_forms(i)
                    response = whole_response(i)
                    fold_out[i] = response
                    fold(i).start()
                    keep(pair, (8, i), response)

                @pl.when(turn)
                def _():
                    late_forms(i)
                    response = whole_response(i)
                    fold(i).wait_recv()
                    keep(pair, (9, i), fold_in[i])
                    beyond = apply(pair, (9, i), fold_out[i])
                    keep(pair, (8, i), beyond)
                    keep(pair, (9, i), response + apply(pair, (7, i), beyond))

            swap(sweep, 1, i).wait_recv()
            near_turn, far_turn = ordered(local[1, i], got[sweep, 1, i])

            def unfed():
                return near_turn + apply(pair, (5, i), far_turn + apply(pair, (4, i), near))

            @pl.when(top)
            def _():
                guess = unfed()
                early(sweep, i).wait_recv()
                early_out[sweep, i] = guess + apply(pair, (8, i), early_in[sweep, i])
                early(sweep, i).start()

            @pl.when(turn)
            def _():
                guess = unfed()
                early(sweep, i).wait_recv()
                local[4, i] = guess + apply(pair, (7, i), early_in[sweep, i])

            @pl.when(has_down)
            def _():
                hop(up, i).wait_recv()

            incoming = arriving[up, i]

            @pl.when(turn)
            def _():
                leaving[down, i] = local[4, i] + apply(pair, (9, i), incoming)
                hop(down, i).start()

            @pl.when(jnp.logical_and(has_up, has_down))
            def _():
                leaving[up, i] = whole + apply(pair, (2, i), incoming)
                hop(up, i).start()

            @pl.when(turn)
            def _():
                arriving[down, i] = early_in[sweep, i] + apply(pair, (8, i), incoming)

            middle = near + apply(pair, (0, i), incoming)
            own_in, foreign_in = ordered(incoming, middle)
            local[2, i] = own_in
            sent[sweep, 2, i] = foreign_in
            swap(sweep, 2, i).start()
            if sweep == 0:

                @pl.when(below)
                def _():
                    late_forms(i)

            far = far_turn + apply(pair, (4, i), middle)
            local[3, i] = far

            @pl.when(below)
            def _():
                local[4, i] = near_turn + apply(pair, (3, i), incoming) + apply(pair, (5, i), far)

        for i in range(half):
            inner_update(mine[i], local[2, i])
        for i in range(half):
            swap(sweep, 2, i).wait_recv()
            inner_update(other[i], got[sweep, 2, i])
        for i in range(half):

            @pl.when(below)
            def _():
                hop(down, i).wait_recv()

            incoming = arriving[down, i]

            @pl.when(jnp.logical_and(below, has_down))
            def _():
                leaving[down, i] = local[4, i] + apply(pair, (7, i), incoming)
                hop(down, i).start()

            middle = local[3, i] + apply(pair, (6, i), incoming)
            foreign_in, own_in = ordered(incoming, middle)
            sent[sweep, 3, i] = foreign_in
            swap(sweep, 3, i).start()
            local[2, i] = own_in

        target = field if sweep < SWEEPS - 1 else out

        def share(a):
            for direction, exists in ((0, ax_up), (1, ax_down)):

                @pl.when(exists)
                def _():
                    side(direction, a).start()

        for i in range(half):
            outer_finish(target, mine[i], local[2, i])
            if sweep < SWEEPS - 1:
                share(mine[i])
        for i in range(half):
            swap(sweep, 3, i).wait_recv()
            outer_finish(target, other[i], got[sweep, 3, i])
            if sweep < SWEEPS - 1:
                share(other[i])

    for i in range(half):
        swap_radial(i).wait_send()
        for c in range(cells):
            swap_block(i, c).wait_send()
        for sweep in range(SWEEPS):
            for kind in range(4):
                swap(sweep, kind, i).wait_send()

            @pl.when(has_up)
            def _():
                hop(2 * sweep, i).wait_send()

            @pl.when(jnp.logical_and(has_up, has_down))
            def _():
                hop(2 * sweep + 1, i).wait_send()

            @pl.when(jnp.logical_not(below))
            def _():
                early(sweep, i).wait_send()

        @pl.when(top)
        def _():
            fold(i).wait_send()

    for direction, exists in ((0, ax_up), (1, ax_down)):

        @pl.when(exists)
        def _():
            for a in mine + other:
                side(direction, a).wait_send()


def on_device(segments, blocks, sources, block_inverse, radial_coupling, axial_coupling):
    stations, cells, species, columns = sources.shape
    half = stations // 2
    assert segments % 2 == 0 and segments >= 6 and stations == WIDTH
    axial = axial_coupling.reshape(-1, species).T
    matrix = pltpu.VMEM((stations, cells, 2, species, species), jnp.bfloat16)
    far_matrix = pltpu.VMEM((half, cells, 2, species, species), jnp.bfloat16)
    square = pltpu.VMEM((3, half, species, species), jnp.float32)
    grid = pltpu.VMEM((stations, cells, species, columns), jnp.float32)
    swaps = pltpu.VMEM((SWEEPS, 4, half, species, columns), jnp.float32)
    slots = pltpu.VMEM((2 * SWEEPS, half, species, columns), jnp.float32)
    earlies = pltpu.VMEM((SWEEPS, half, species, columns), jnp.float32)
    fold = pltpu.VMEM((half, species, species), jnp.float32)
    sems = [
        pltpu.SemaphoreType.DMA(shape)
        for shape in ((cells + 1, half), (SWEEPS, 4, half), (2 * SWEEPS, half), (2, stations), (SWEEPS, half), (half,))
        for side in range(2)
    ]
    spec = pl.BlockSpec(memory_space=pltpu.VMEM)
    raw = pl.BlockSpec(memory_space=pl.ANY)
    sems.append(pltpu.SemaphoreType.DMA((2,)))
    return pl.pallas_call(
        functools.partial(kernel, segments, blocks),
        out_shape=jax.ShapeDtypeStruct(sources.shape, jnp.float32),
        in_specs=[raw, raw, spec, spec],
        out_specs=spec,
        scratch_shapes=[
            grid,
            pltpu.VMEM(block_inverse.shape, jnp.float32),
            matrix,
            matrix,
            matrix,
            pltpu.VMEM((10, half, 2, species, species), jnp.bfloat16),
            far_matrix,
            far_matrix,
            pltpu.VMEM((half, cells, species, species), jnp.float32),
            pltpu.VMEM((half, *radial_coupling.shape[1:]), jnp.float32),
            square,
            square,
            fold,
            fold,
            grid,
            grid,
            grid,
            grid,
            grid,
            swaps,
            swaps,
            pltpu.VMEM((5, half, species, columns), jnp.float32),
            slots,
            slots,
            earlies,
            earlies,
            *sems,
        ],
        compiler_params=pltpu.CompilerParams(
            collective_id=0, has_side_effects=True, vmem_limit_bytes=63 << 20
        ),
    )(sources, block_inverse, radial_coupling, axial)


def solution(mesh):
    placed = P("ax", "rad", None, None)
    return jax.shard_map(
        functools.partial(on_device, mesh.shape["rad"], mesh.shape["ax"]),
        mesh=mesh,
        in_specs=(placed,) * 4,
        out_specs=placed,
        check_vma=False,
    )
```
